32 devices in a mesh: dp: 8 (over z, y), head: 4 (over x, core).
Axes of the slice: x: 2, y: 2, z: 4, core: 2. Of those that a mesh axis runs over, the one named last changes fastest.
Arguments:
- tokens: bfloat16 [2, 32, 512, 768], P(None, ('dp', 'head')), may hold values from -6 to 6
- lengths: int32 [2, 32], P(None, 'dp'), may hold values from 1 to 512, as said below
- cotangent: bfloat16 [2, 32, 512, 768], P(None, ('dp', 'head')), may hold values from -12 to 12
- qkv_weight: bfloat16 [768, 2304], P('dp', 'head'), may hold values from -0.3125 to 0.3125
- qv_shift: bfloat16 [12, 128], P('head', 'dp'), may hold values from -3 to 3
- proj_weight: bfloat16 [768, 768], P(('dp', 'head')), may hold values from -0.875 to 0.875
- proj_shift: bfloat16 [768], P(('dp', 'head')), may hold values from -3 to 3
- first_gain: bfloat16 [768], P(('dp', 'head')), may hold values from 0.5 to 1.5
- first_shift: bfloat16 [768], P(('dp', 'head')), may hold values from -1.75 to 1.75
- inner_weight: bfloat16 [768, 3072], P(('dp', 'head')), may hold values from -0.21875 to 0.21875
- inner_shift: bfloat16 [3072], P(('dp', 'head')), may hold values from -3 to 3
- outer_weight: bfloat16 [3072, 768], P(('dp', 'head')), may hold values from -0.21875 to 0.21875
- outer_shift: bfloat16 [768], P(('dp', 'head')), may hold values from -3 to 3
- second_gain: bfloat16 [768], P(('dp', 'head')), may hold values from 0.5 to 1.5
- second_shift: bfloat16 [768], P(('dp', 'head')), may hold values from -1.75 to 1.75
Outputs:
- layer_output: bfloat16 [2, 32, 512, 768], P(None, ('dp', 'head'))
- tokens_gradient: bfloat16 [2, 32, 512, 768], P(None, ('dp', 'head'))
- qkv_gradient: float32 [768, 2304], P('dp', 'head')
- qvshift_gradient: float32 [12, 128], P('head', 'dp')
- proj_gradient: float32 [768, 768], P(('dp', 'head'))
- projshift_gradient: float32 [768], P(('dp', 'head'))
- firstgain_gradient: float32 [768], P(('dp', 'head'))
- firstshift_gradient: float32 [768], P(('dp', 'head'))
- inner_gradient: float32 [768, 3072], P(('dp', 'head'))
- innershift_gradient: float32 [3072], P(('dp', 'head'))
- outer_gradient: float32 [3072, 768], P(('dp', 'head'))
- outershift_gradient: float32 [768], P(('dp', 'head'))
- secondgain_gradient: float32 [768], P(('dp', 'head'))
- secondshift_gradient: float32 [768], P(('dp', 'head'))
The draws below stay inside these ranges and needn't reach their ends.
Inputs may be any that keep to these rules, and one draw needn't show every extreme that they name: lengths[m, s] is the number of live slots at the start of row s of micro-batch m; the other slots are padding. Lengths are mixed: some row has all 512 slots live, others about a third of them.
All inputs are finite; a program needn't handle non-finite values.
Results may differ from the reference program's by a relative error of at most 0.018.
Values may be sent and summed in bfloat16 or wider, within the bound.
No kernel may reach another device: no remote copies, remote signals or barrier semaphores. Data moves between devices by JAX's collectives and lax.ppermute only.
A program may use at most 192 MiB of HBM per device.

```python
import math
import jax
import jax.numpy as jnp
from jax import lax

D = 768
HEADS = 12
DH = 64
FF = 3072
SLOTS = 512
MB = 2
SEQS = 32


def draw_lengths(key, part):
    key_divisor, key_jitter, key_choice = jax.random.split(key, 3)
    divisor = jax.random.randint(key_divisor, (MB, SEQS), 1, 4)
    baseline = SLOTS // divisor
    jitter = jax.random.randint(key_jitter, (MB, SEQS), 0, 4) * (baseline // 8)
    counts_flat = (baseline - jitter).reshape(-1)
    chosen = jax.random.randint(key_choice, (), 0, MB * SEQS)
    counts_flat = counts_flat.at[chosen].set(SLOTS)
    return counts_flat.reshape(MB, SEQS).astype(jnp.int32)


def raised(values, key, source, target, blocks, factor):
    owner, partner = [(jnp.arange(values.shape[axis_at]) // (values.shape[axis_at] // blocks)).reshape([-1 if axis == axis_at else 1 for axis in range(values.ndim)]) for axis_at in (source, target)]
    chosen = jax.random.permutation(key, blocks)[partner]
    strong = (owner == chosen) | (owner == (partner + blocks // 2) % blocks)
    return jnp.where(strong, factor * values, values)


def levels(stream_key, shape, cuts, low, high):
    loudness, own = 1.0, jax.random.fold_in(stream_key, 6)
    for dim, shards_of in cuts:
        heights = jnp.exp(jax.random.uniform(jax.random.fold_in(own, dim), (shards_of,), jnp.float32, low / len(cuts), high / len(cuts)))
        loudness = loudness * jnp.repeat(heights, shape[dim] // shards_of).reshape([-1 if axis == dim else 1 for axis in range(len(shape))])
    return loudness


def noise(key, shape, scale, most, cuts=(), held_as=jnp.bfloat16):
    values = scale * jax.random.normal(key, shape, jnp.float32)
    if cuts:
        values = values * levels(key, shape, cuts, -0.22, 0.18)
    return jnp.clip(values, -most, most).astype(held_as)


def heavy_noise(stream_key, dims, width, reach, cuts, heavy, held_as=jnp.bfloat16):
    entries = width * jax.random.normal(stream_key, dims, jnp.float32)
    if cuts:
        entries = entries * levels(stream_key, dims, cuts, -0.22, 0.18)
    return jnp.clip(raised(entries, jax.random.fold_in(stream_key, 3), *heavy), -reach, reach).astype(held_as)


def setup_inputs(seed: int = 0) -> dict:
    splits = jax.random.split(jax.random.key(seed), 16)
    tokens = noise(splits[0], (MB, SEQS, SLOTS, D), 1.0, 6.0, ((1, 32),))
    lengths = draw_lengths(jax.random.fold_in(splits[15], 71), 0)
    cotangent = heavy_noise(splits[2], (MB, SEQS, SLOTS, D), 1.0, 12.0, ((1, 32),), (1, 3, 32, 2.75))
    qkv_weight = noise(splits[3], (D, 3 * D), (D // 2) ** -0.5, 0.3125, ((0, 8), (1, 4)))
    qv_shift = noise(splits[4], (HEADS, 2 * DH), 0.5, 3.0, ((0, 4), (1, 8)))
    proj_weight = noise(splits[5], (D, D), (D // 16) ** -0.5, 0.875, ((0, 32),))
    proj_shift = noise(splits[6], (D,), 0.5, 3.0, ((0, 32),))
    first_gain = jnp.clip(1.0 + 0.1 * jax.random.normal(splits[7], (D,), jnp.float32), 0.5, 1.5).astype(jnp.bfloat16)
    first_shift = noise(splits[8], (D,), 0.3, 1.75, ((0, 32),))
    inner_weight = noise(splits[9], (D, FF), D ** -0.5, 0.21875, ((0, 32),))
    inner_shift = noise(splits[10], (FF,), 0.5, 3.0, ((0, 32),))
    outer_weight = noise(splits[11], (FF, D), (FF // 4) ** -0.5, 0.21875, ((0, 32),))
    outer_shift = noise(splits[12], (D,), 0.5, 3.0, ((0, 32),))
    second_gain = jnp.clip(1.0 + 0.1 * jax.random.normal(splits[13], (D,), jnp.float32), 0.5, 1.5).astype(jnp.bfloat16)
    second_shift = noise(splits[14], (D,), 0.3, 1.75, ((0, 32),))
    return {"tokens": tokens, "lengths": lengths, "cotangent": cotangent, "qkv_weight": qkv_weight, "qv_shift": qv_shift, "proj_weight": proj_weight, "proj_shift": proj_shift, "first_gain": first_gain, "first_shift": first_shift, "inner_weight": inner_weight, "inner_shift": inner_shift, "outer_weight": outer_weight, "outer_shift": outer_shift, "second_gain": second_gain, "second_shift": second_shift}


EPSILON = 1e-12
PRECISE = lax.Precision.HIGHEST

@jax.custom_vjp
def low(v):
    return lax.optimization_barrier(v.astype(jnp.bfloat16)).astype(jnp.float32)

@jax.custom_vjp
def low_back(v):
    return v

def low_keep(v):
    return (low(v), None)

def low_pass(kept, grad):
    return (grad,)

def back_keep(v):
    return (v, None)

def back_low(kept, grad):
    return (low(grad),)
low.defvjp(low_keep, low_pass)
low_back.defvjp(back_keep, back_low)

def layer_norm(hidden, scale_gain, offset):
    center = hidden - lax.optimization_barrier(jnp.mean(hidden, axis=-1, keepdims=True))
    spread = lax.optimization_barrier(jnp.mean(center * center, axis=-1, keepdims=True))
    return center * lax.rsqrt(spread + EPSILON) * scale_gain + offset

def encode_group(tokens_block, live_block, params):
    qkv_weight, qv_shift, proj_weight, proj_shift, first_gain, first_shift, inner_weight, inner_shift, outer_weight, outer_shift, second_gain, second_shift = params
    groups = tokens_block.shape[0]
    packed = jnp.einsum('gsd,de->gse', tokens_block, qkv_weight, precision=PRECISE)
    packed = packed.reshape(groups, SLOTS, HEADS, 3, DH)
    queries = low_back(low(packed[:, :, :, 0, :] + qv_shift[:, :DH]))
    keyset = low_back(low(packed[:, :, :, 1, :]))
    values = low_back(low(packed[:, :, :, 2, :] + qv_shift[:, DH:]))
    scores = low_back(jnp.einsum('gqhd,gkhd->ghqk', queries, keyset, precision=PRECISE) * DH ** (-0.5))
    scores = jnp.where(live_block[:, None, None, :] > 0.5, scores, -1e+30)
    highest = lax.optimization_barrier(jnp.max(scores, axis=-1, keepdims=True))
    exponent = jnp.exp(scores - highest)
    soft_low = low(exponent / lax.optimization_barrier(jnp.sum(exponent, axis=-1, keepdims=True)))
    context = jnp.einsum('ghqk,gkhd->gqhd', soft_low, values, precision=PRECISE)
    context = low_back(low(context.reshape(groups, SLOTS, D)))
    attended = low_back(jnp.einsum('gsd,de->gse', context, proj_weight, precision=PRECISE) + proj_shift)
    normed = layer_norm(tokens_block + attended, first_gain, first_shift)
    inner_pre = low_back(jnp.einsum('gsd,df->gsf', low(normed), inner_weight, precision=PRECISE) + inner_shift)
    active = low(jax.nn.gelu(inner_pre, approximate=False))
    outer_pre = low_back(jnp.einsum('gsf,fd->gsd', active, outer_weight, precision=PRECISE) + outer_shift)
    return layer_norm(normed + outer_pre, second_gain, second_shift)

def reference(tokens, lengths, cotangent, qkv_weight, qv_shift, proj_weight, proj_shift, first_gain, first_shift, inner_weight, inner_shift, outer_weight, outer_shift, second_gain, second_shift):
    params = tuple((weight.astype(jnp.float32) for weight in (qkv_weight, qv_shift, proj_weight, proj_shift, first_gain, first_shift, inner_weight, inner_shift, outer_weight, outer_shift, second_gain, second_shift)))
    groups = math.gcd(MB * SEQS, max(1, 4096 // SLOTS))
    blocks = MB * SEQS // groups
    inputs_all = tokens.astype(jnp.float32).reshape(blocks, groups, SLOTS, D)
    slot_ids = jnp.arange(SLOTS, dtype=jnp.int32)
    live_slots = (slot_ids[None, :] < lengths.reshape(-1).astype(jnp.int32)[:, None]).astype(jnp.float32)
    live_slots = live_slots.reshape(blocks, groups, SLOTS)

    def forward(inputs, weights):

        def one_block(block_pair):
            return jax.checkpoint(encode_group)(block_pair[0], block_pair[1], weights)
        return lax.map(one_block, (inputs, live_slots))
    output, pullback = jax.vjp(forward, inputs_all, params)
    upstream = cotangent.astype(jnp.float32).reshape(inputs_all.shape) * live_slots[..., None]
    input_grad, weight_grads = pullback(upstream)
    full_shape = tokens.shape
    return (output.reshape(full_shape).astype(jnp.bfloat16), input_grad.reshape(full_shape).astype(jnp.bfloat16), weight_grads[0], weight_grads[1], weight_grads[2], weight_grads[3], weight_grads[4], weight_grads[5], weight_grads[6], weight_grads[7], weight_grads[8], weight_grads[9], weight_grads[10], weight_grads[11])
```

```python
import jax
import jax.numpy as jnp
from jax import lax
from jax.experimental import pallas as pl
from jax.experimental.pallas import tpu as pltpu
from jax.sharding import PartitionSpec as P

DH = 64
EPSILON = 1e-12
AXES = ("dp", "head")
LOW = jnp.bfloat16
F32 = jnp.float32


def flat(z, y, x, c):
    return ((z * 2 + y) * 2 + x) * 2 + c


def move(value, dz=0, dy=0, dx=0, dc=0):
    pairs = [
        (flat(z, y, x, c), flat((z + dz) % 4, y ^ dy, x ^ dx, c ^ dc))
        for z in range(4)
        for y in range(2)
        for x in range(2)
        for c in range(2)
    ]
    return lax.ppermute(value, AXES, pairs)


def coords():
    dp, head = lax.axis_index("dp"), lax.axis_index("head")
    return jnp.stack([dp // 2, dp % 2, head // 2, head % 2]).astype(jnp.int32)


PIECES = [
    (ry, rx, rc, first, count)
    for rc in (0, 1)
    for ry, rx, first, count in ((0, 0, 0, 4), (1, 0, 0, 4), (0, 1, 0, 4), (1, 1, 0, 2), (1, 1, 2, 2))
]


def gather_pieces(shard):
    own = shard[None]
    plane = jnp.concatenate([own] + [move(own, dz=k) for k in (1, 2, 3)], axis=0)
    from_y = move(plane, dy=1)
    from_x = move(plane, dx=1)
    far_a = move(from_y[:2], dx=1)
    far_b = move(from_x[2:], dy=1)
    mine = [plane, from_y, from_x, far_a, far_b]
    return mine + [move(piece, dc=1) for piece in mine]


def assemble(shard, where):
    pieces = gather_pieces(shard)

    def body(where_ref, *refs):
        ins, out, sems = refs[: len(PIECES)], refs[len(PIECES)], refs[len(PIECES) + 1]
        z, y, x, c = (where_ref[i] for i in range(4))
        copies = []
        for ref, (ry, rx, rc, first, count) in zip(ins, PIECES):
            for k in range(count):
                source_z = lax.rem(z + 4 - (first + k), 4)
                target = flat(source_z, y ^ ry, x ^ rx, c ^ rc)
                copy = pltpu.make_async_copy(ref.at[k], out.at[target], sems.at[len(copies)])
                copy.start()
                copies.append(copy)
        for copy in copies:
            copy.wait()

    return pl.pallas_call(
        body,
        out_shape=jax.ShapeDtypeStruct((32,) + shard.shape, shard.dtype),
        in_specs=[pl.BlockSpec(memory_space=pltpu.SMEM)] + [pl.BlockSpec(memory_space=pl.ANY)] * len(pieces),
        out_specs=pl.BlockSpec(memory_space=pl.ANY),
        scratch_shapes=[pltpu.SemaphoreType.DMA((32,))],
        name="assemble",
    )(where, *pieces)


def split_parts(full, where):
    def body(where_ref, full_ref, keep_ref, send_ref, sems):
        z, y, x, c = (where_ref[i] for i in range(4))
        copies = []
        for rc, out in ((0, keep_ref), (1, send_ref)):
            for ry in (0, 1):
                for rx in (0, 1):
                    for rz in range(4):
                        source = flat(lax.rem(z + rz, 4), y ^ ry, x ^ rx, c ^ rc)
                        copy = pltpu.make_async_copy(full_ref.at[source], out.at[ry, rx, rz], sems.at[len(copies)])
                        copy.start()
                        copies.append(copy)
        for copy in copies:
            copy.wait()

    half = jax.ShapeDtypeStruct((2, 2, 4) + full.shape[1:], full.dtype)
    return pl.pallas_call(
        body,
        out_shape=(half, half),
        in_specs=[pl.BlockSpec(memory_space=pltpu.SMEM), pl.BlockSpec(memory_space=pl.ANY)],
        out_specs=(pl.BlockSpec(memory_space=pl.ANY), pl.BlockSpec(memory_space=pl.ANY)),
        scratch_shapes=[pltpu.SemaphoreType.DMA((32,))],
        name="split_parts",
    )(where, full)


def reduce_parts(kept, sent):
    kind = kept.dtype

    def add(first, *rest):
        total = first.astype(F32)
        for term in rest:
            total = total + term.astype(F32)
        return total

    here = add(kept, move(sent, dc=1)).astype(kind)
    far = here[1, 1]
    near_y, near_x = here[1, 0], here[0, 1]
    via_x = move(far[:2], dx=1)
    via_y = move(far[2:], dy=1)
    to_y = jnp.concatenate([add(near_y[:2], via_x).astype(kind), near_y[2:]], axis=0)
    to_x = jnp.concatenate([near_x[:2], add(near_x[2:], via_y).astype(kind)], axis=0)
    plane = add(here[0, 0], move(to_y, dy=1), move(to_x, dx=1))
    low = plane.astype(kind)
    return add(plane[0], *[move(low[k], dz=k) for k in (1, 2, 3)])


def norm_stats(hidden):
    center = hidden - jnp.mean(hidden, axis=-1, keepdims=True)
    spread = jnp.mean(center * center, axis=-1, keepdims=True)
    inverse = lax.rsqrt(spread + EPSILON)
    return center * inverse, inverse


def norm_back(grad_hat, hat, inverse):
    return inverse * (
        grad_hat
        - jnp.mean(grad_hat, axis=-1, keepdims=True)
        - hat * jnp.mean(grad_hat * hat, axis=-1, keepdims=True)
    )


def gelu_both(values):
    half = 0.5 * (1.0 + lax.erf(values * 0.7071067811865476))
    slope = half + values * jnp.exp(-0.5 * values * values) * 0.3989422804014327
    return values * half, slope


def mm(a, b, dims):
    return lax.dot_general(a, b, (dims, ((), ())), preferred_element_type=F32)


def layer(tokens, lengths, cotangent, weights):
    qkv, qv_shift, proj, proj_shift, gain_one, shift_one, inner, inner_shift, outer, outer_shift, gain_two, shift_two = weights
    rows, slots, features = tokens.shape
    groups, _, width = qkv.shape
    per = width // (3 * DH)
    heads = groups * per
    count = rows * slots
    live = jnp.arange(slots, dtype=jnp.int32)[None, :] < lengths[:, None]
    packed = jnp.einsum("bsd,gde->bsge", tokens, qkv, preferred_element_type=F32)
    packed = packed.reshape(rows, slots, heads, 3, DH)
    queries = (packed[:, :, :, 0] + qv_shift[:, :DH]).astype(LOW)
    keyset = packed[:, :, :, 1].astype(LOW)
    values = (packed[:, :, :, 2] + qv_shift[:, DH:]).astype(LOW)

    def scored(q, k):
        scores = jnp.einsum("bqhd,bkhd->bhqk", q, k, preferred_element_type=F32) * DH**-0.5
        return jnp.where(live[:, None, None, :], scores, -1e30)

    scores = scored(queries, keyset)
    highest = jnp.max(scores, axis=-1, keepdims=True)
    raised = jnp.exp(scores - highest)
    soft_low = (raised / jnp.sum(raised, axis=-1, keepdims=True)).astype(LOW)
    context = jnp.einsum("bhqk,bkhd->bqhd", soft_low, values, preferred_element_type=F32)
    context = context.astype(LOW).reshape(count, features)
    flat_tokens = tokens.reshape(count, features)
    first = flat_tokens.astype(F32) + mm(context, proj, ((1,), (0,))) + proj_shift
    hat_one, inverse_one = norm_stats(first)
    normed = hat_one * gain_one + shift_one
    normed_low = normed.astype(LOW)
    active, slope = gelu_both(mm(normed_low, inner, ((1,), (0,))) + inner_shift)
    active_low = active.astype(LOW)
    second = normed + mm(active_low, outer, ((1,), (0,))) + outer_shift
    hat_two, inverse_two = norm_stats(second)
    result = (hat_two * gain_two + shift_two).astype(LOW).reshape(tokens.shape)
    upstream = cotangent.reshape(count, features).astype(F32) * live.reshape(count, 1).astype(F32)
    gain_two_grad = jnp.sum(upstream * hat_two, axis=0)
    shift_two_grad = jnp.sum(upstream, axis=0)
    second_grad = norm_back(upstream * gain_two, hat_two, inverse_two)
    outer_low = second_grad.astype(LOW)
    outer_grad = mm(active_low, outer_low, ((0,), (0,))).astype(LOW)
    outer_shift_grad = jnp.sum(outer_low.astype(F32), axis=0)
    inner_low = (mm(outer_low, outer, ((1,), (1,))) * slope).astype(LOW)
    inner_grad = mm(normed_low, inner_low, ((0,), (0,))).astype(LOW)
    inner_shift_grad = jnp.sum(inner_low.astype(F32), axis=0)
    normed_grad = second_grad + mm(inner_low, inner, ((1,), (1,)))
    gain_one_grad = jnp.sum(normed_grad * hat_one, axis=0)
    shift_one_grad = jnp.sum(normed_grad, axis=0)
    first_grad = norm_back(normed_grad * gain_one, hat_one, inverse_one)
    attended_low = first_grad.astype(LOW)
    proj_grad = mm(context, attended_low, ((0,), (0,))).astype(LOW)
    proj_shift_grad = jnp.sum(attended_low.astype(F32), axis=0)
    context_grad = mm(attended_low, proj, ((1,), (1,))).astype(LOW).reshape(rows, slots, heads, DH)
    soft = soft_low.astype(F32)
    soft_grad = jnp.einsum("bqhd,bkhd->bhqk", context_grad, values, preferred_element_type=F32)
    score_low = (soft * (soft_grad - jnp.sum(soft * soft_grad, axis=-1, keepdims=True))).astype(LOW)
    query_grad = jnp.einsum("bhqk,bkhd->bqhd", score_low, keyset, preferred_element_type=F32) * DH**-0.5
    key_grad = jnp.einsum("bhqk,bqhd->bkhd", score_low, queries, preferred_element_type=F32) * DH**-0.5
    value_grad = jnp.einsum("bhqk,bqhd->bkhd", soft_low, context_grad, preferred_element_type=F32)
    packed_grad = jnp.stack([query_grad, key_grad, value_grad], axis=3).astype(LOW)
    shift_grad = jnp.sum(packed_grad.astype(F32), axis=(0, 1))
    qv_shift_grad = jnp.concatenate([shift_grad[:, 0], shift_grad[:, 2]], axis=1)
    packed_grad = packed_grad.reshape(count, groups, width)
    qkv_grad = jnp.einsum("nd,nge->gde", flat_tokens, packed_grad, preferred_element_type=F32).astype(LOW)
    input_grad = first_grad + jnp.einsum("nge,gde->nd", packed_grad, qkv, preferred_element_type=F32)
    input_grad = input_grad.astype(LOW).reshape(tokens.shape)
    grads = (
        qkv_grad, qv_shift_grad, proj_grad, proj_shift_grad, gain_one_grad, shift_one_grad,
        inner_grad, inner_shift_grad, outer_grad, outer_shift_grad, gain_two_grad, shift_two_grad,
    )
    return result, input_grad, grads


def on_device(*args):
    tokens, lengths, cotangent = args[:3]
    params = args[3:]
    qkv_weight, qv_shift, proj_weight, proj_shift, first_gain, first_shift = params[:6]
    inner_weight, inner_shift, outer_weight, outer_shift, second_gain, second_shift = params[6:]
    micro, local, slots, features = tokens.shape
    dp, groups = lax.axis_size("dp"), lax.axis_size("head")
    staged = (dp, groups) == (8, 4)
    position = lax.axis_index("head")
    where = coords()
    own = lax.dynamic_slice_in_dim(lengths, position * local, local, 1).reshape(micro * local)
    rows = tokens.reshape(micro * local, slots, features)
    upstream = cotangent.reshape(micro * local, slots, features)

    vectors = [proj_shift, first_gain, first_shift, outer_shift, second_gain, second_shift, inner_shift, qv_shift.reshape(-1)]
    lens = [v.shape[0] for v in vectors]
    total = sum(lens)
    padded = -(-total // 1024) * 1024
    small = jnp.pad(jnp.concatenate(vectors), (0, padded - total)).reshape(8, padded // 8)

    def everyone(shard):
        if staged:
            return assemble(shard, where)
        return lax.all_gather(shard, AXES, axis=0)

    qkv_all = everyone(qkv_weight)
    small_all = everyone(small).reshape(dp * groups, padded)
    proj = everyone(proj_weight).reshape(-1, features)
    inner = everyone(inner_weight).reshape(features, -1)
    outer = everyone(outer_weight).reshape(-1, features)
    depth, width = qkv_weight.shape
    qkv = qkv_all.reshape(dp, groups, depth, width).swapaxes(0, 1).reshape(groups, dp * depth, width)
    pieces, at = [], 0
    for size in lens:
        pieces.append(small_all[:, at : at + size].astype(F32))
        at += size
    full = [p.reshape(-1) for p in pieces[:-1]]
    shift = pieces[-1].reshape((dp, groups) + qv_shift.shape).transpose(1, 2, 0, 3).reshape(-1, 2 * DH)
    weights = (qkv, shift, proj, full[0], full[1], full[2], inner, full[6], outer, full[3], full[4], full[5])
    result, input_grad, grads = layer(rows, own, upstream, weights)
    (
        qkv_grad, qv_shift_grad, proj_grad, proj_shift_grad, gain_one_grad, shift_one_grad,
        inner_grad, inner_shift_grad, outer_grad, outer_shift_grad, gain_two_grad, shift_two_grad,
    ) = grads

    def owner(grad):
        if staged:
            return reduce_parts(*split_parts(grad, where))
        parts = lax.all_to_all(grad, AXES, 0, 0, tiled=True)
        return jnp.sum(parts.astype(F32), axis=0)

    devices = dp * groups
    outer_out = owner(outer_grad.reshape((devices,) + outer_weight.shape))
    inner_out = owner(inner_grad.reshape((devices,) + inner_weight.shape))
    proj_out = owner(proj_grad.reshape((devices,) + proj_weight.shape))
    qkv_blocks = qkv_grad.reshape(groups, dp, depth, width).swapaxes(0, 1)
    qkv_out = owner(qkv_blocks.reshape(devices, depth, width))
    shift_blocks = qv_shift_grad.reshape(groups, qv_shift.shape[0], dp, qv_shift.shape[1]).transpose(2, 0, 1, 3)
    vector_grads = [proj_shift_grad, gain_one_grad, shift_one_grad, outer_shift_grad, gain_two_grad, shift_two_grad, inner_shift_grad, shift_blocks]
    small_grad = jnp.concatenate([g.reshape(devices, -1) for g in vector_grads], axis=1)
    small_grad = jnp.pad(small_grad, ((0, 0), (0, padded - total))).reshape(devices, 8, padded // 8)
    small_out = owner(small_grad).reshape(padded)
    outs, at = [], 0
    for size in lens:
        outs.append(small_out[at : at + size])
        at += size
    return (
        result.reshape(tokens.shape), input_grad.reshape(tokens.shape),
        qkv_out, outs[7].reshape(qv_shift.shape), proj_out, outs[0], outs[1], outs[2],
        inner_out, outs[6], outer_out, outs[3], outs[4], outs[5],
    )


def solution(mesh):
    both = ("dp", "head")
    rows, whole = P(both), P(both, None)
    data = P(None, both, None, None)
    params = (P("dp", "head"), P("head", "dp"), whole, rows, rows, rows, whole, rows, whole, rows, rows, rows)
    in_specs = (data, P(None, "dp"), data) + params
    out_specs = (data, data) + params
    return jax.shard_map(on_device, mesh=mesh, in_specs=in_specs, out_specs=out_specs, check_vma=False)
```

```python
import jax
import jax.numpy as jnp
from jax import lax
from jax.experimental import pallas as pl
from jax.experimental.pallas import tpu as pltpu
from jax.sharding import PartitionSpec as P

DH = 64
EPSILON = 1e-12
AXES = ("dp", "head")
LOW = jnp.bfloat16
F32 = jnp.float32


Z_FAR, Z_NEAR, Y, X, CORE = 16, 8, 4, 2, 1


def move(value, bit):
    return lax.ppermute(value, AXES, [(d, d ^ bit) for d in range(32)])


PLANE = [0, Z_NEAR, Z_FAR, Z_FAR | Z_NEAR]
OFFSETS = PLANE + [Y | p for p in PLANE] + [X | p for p in PLANE] + [Y | X | p for p in PLANE]


def gather_half(shard):
    own = shard[None]
    pair = jnp.concatenate([own, move(own, Z_NEAR)], axis=0)
    plane = jnp.concatenate([pair, move(pair, Z_FAR)], axis=0)
    from_y = move(plane, Y)
    from_x = move(plane, X)
    far_a = move(from_y[:2], X)
    far_b = move(from_x[2:], Y)
    return jnp.concatenate([plane, from_y, from_x, far_a, far_b], axis=0)


def device_index():
    return (lax.axis_index("dp") * lax.axis_size("head") + lax.axis_index("head")).astype(jnp.int32).reshape(1)


def assemble(shard, me, outs, targets):
    mine = gather_half(shard)
    theirs = move(mine, CORE)

    def body(me_ref, mine_ref, theirs_ref, *rest):
        out_refs, sems = rest[:-1], rest[-1]
        copies = []
        for core, ref in ((0, mine_ref), (CORE, theirs_ref)):
            for k, offset in enumerate(OFFSETS):
                for source, target in targets(ref.at[k], out_refs, me_ref[0] ^ (offset | core)):
                    copy = pltpu.make_async_copy(source, target, sems.at[len(copies)])
                    copy.start()
                    copies.append(copy)
        for copy in copies:
            copy.wait()

    hbm = pl.BlockSpec(memory_space=pl.ANY)
    return pl.pallas_call(
        body,
        out_shape=outs,
        in_specs=[pl.BlockSpec(memory_space=pltpu.SMEM), hbm, hbm],
        out_specs=[pl.BlockSpec(memory_space=pltpu.VMEM)] * len(outs),
        scratch_shapes=[pltpu.SemaphoreType.DMA((32 * len(outs),))],
        name="assemble",
    )(me, mine, theirs)


def split_parts(fulls, me, block, sources):
    def body(me_ref, *rest):
        full_refs, (keep_ref, send_ref, sems) = rest[: len(fulls)], rest[len(fulls) :]
        copies = []
        for core, out in ((0, keep_ref), (CORE, send_ref)):
            for k, offset in enumerate(OFFSETS):
                for source, target in sources(full_refs, out.at[k], me_ref[0] ^ (offset | core)):
                    copy = pltpu.make_async_copy(source, target, sems.at[len(copies)])
                    copy.start()
                    copies.append(copy)
        for copy in copies:
            copy.wait()

    half = jax.ShapeDtypeStruct((16,) + block, LOW)
    hbm = pl.BlockSpec(memory_space=pl.ANY)
    return pl.pallas_call(
        body,
        out_shape=(half, half),
        in_specs=[pl.BlockSpec(memory_space=pltpu.SMEM)] + [pl.BlockSpec(memory_space=pltpu.VMEM)] * len(fulls),
        out_specs=(hbm, hbm),
        scratch_shapes=[pltpu.SemaphoreType.DMA((32 * len(fulls),))],
        name="split_parts",
    )(me, *fulls)


def add(first, *rest):
    total = first.astype(F32)
    for term in rest:
        total = total + term.astype(F32)
    return total


def reduce_parts(kept, sent):
    here = add(kept, move(sent, CORE)).astype(LOW)
    plane, near_y, near_x, far = here[:4], here[4:8], here[8:12], here[12:]
    via_x = move(far[:2], X)
    via_y = move(far[2:], Y)
    to_y = jnp.concatenate([add(near_y[:2], via_x).astype(LOW), near_y[2:]], axis=0)
    to_x = jnp.concatenate([near_x[:2], add(near_x[2:], via_y).astype(LOW)], axis=0)
    plane = add(plane, move(to_y, Y), move(to_x, X))
    pair = add(plane[:2], move(plane[2:].astype(LOW), Z_FAR))
    return add(pair[0], move(pair[1].astype(LOW), Z_NEAR))


def norm_stats(hidden):
    center = hidden - jnp.mean(hidden, axis=-1, keepdims=True)
    spread = jnp.mean(center * center, axis=-1, keepdims=True)
    inverse = lax.rsqrt(spread + EPSILON)
    return center * inverse, inverse


def norm_back(grad_hat, hat, inverse):
    return inverse * (
        grad_hat
        - jnp.mean(grad_hat, axis=-1, keepdims=True)
        - hat * jnp.mean(grad_hat * hat, axis=-1, keepdims=True)
    )


def gelu_both(values):
    half = 0.5 * (1.0 + lax.erf(values * 0.7071067811865476))
    slope = half + values * jnp.exp(-0.5 * values * values) * 0.3989422804014327
    return values * half, slope


def mm(a, b, dims):
    return lax.dot_general(a, b, (dims, ((), ())), preferred_element_type=F32)


def layer(tokens, lengths, cotangent, weights):
    qkv, qv_shift, proj, proj_shift, gain_one, shift_one, inner, inner_shift, outer, outer_shift, gain_two, shift_two = weights
    rows, slots, features = tokens.shape
    groups, _, width = qkv.shape
    per = width // (3 * DH)
    heads = groups * per
    count = rows * slots
    live = jnp.arange(slots, dtype=jnp.int32)[None, :] < lengths[:, None]
    packed = jnp.einsum("bsd,gde->bsge", tokens, qkv, preferred_element_type=F32)
    packed = packed.reshape(rows, slots, heads, 3, DH)
    queries = (packed[:, :, :, 0] + qv_shift[:, :DH]).astype(LOW)
    keyset = packed[:, :, :, 1].astype(LOW)
    values = (packed[:, :, :, 2] + qv_shift[:, DH:]).astype(LOW)

    def scored(q, k):
        scores = jnp.einsum("bqhd,bkhd->bhqk", q, k, preferred_element_type=F32) * DH**-0.5
        return jnp.where(live[:, None, None, :], scores, -1e30)

    scores = scored(queries, keyset)
    highest = jnp.max(scores, axis=-1, keepdims=True)
    raised = jnp.exp(scores - highest)
    soft_low = (raised / jnp.sum(raised, axis=-1, keepdims=True)).astype(LOW)
    context = jnp.einsum("bhqk,bkhd->bqhd", soft_low, values, preferred_element_type=F32)
    context = context.astype(LOW).reshape(count, features)
    flat_tokens = tokens.reshape(count, features)
    first = flat_tokens.astype(F32) + mm(context, proj, ((1,), (0,))) + proj_shift
    hat_one, inverse_one = norm_stats(first)
    normed = hat_one * gain_one + shift_one
    normed_low = normed.astype(LOW)
    active, slope = gelu_both(mm(normed_low, inner, ((1,), (0,))) + inner_shift)
    active_low = active.astype(LOW)
    second = normed + mm(active_low, outer, ((1,), (0,))) + outer_shift
    hat_two, inverse_two = norm_stats(second)
    result = (hat_two * gain_two + shift_two).astype(LOW).reshape(tokens.shape)
    upstream = cotangent.reshape(count, features).astype(F32) * live.reshape(count, 1).astype(F32)
    gain_two_grad = jnp.sum(upstream * hat_two, axis=0)
    shift_two_grad = jnp.sum(upstream, axis=0)
    second_grad = norm_back(upstream * gain_two, hat_two, inverse_two)
    outer_low = second_grad.astype(LOW)
    outer_grad = mm(active_low, outer_low, ((0,), (0,))).astype(LOW)
    outer_shift_grad = jnp.sum(outer_low.astype(F32), axis=0)
    inner_low = (mm(outer_low, outer, ((1,), (1,))) * slope).astype(LOW)
    inner_grad = mm(normed_low, inner_low, ((0,), (0,))).astype(LOW)
    inner_shift_grad = jnp.sum(inner_low.astype(F32), axis=0)
    normed_grad = second_grad + mm(inner_low, inner, ((1,), (1,)))
    gain_one_grad = jnp.sum(normed_grad * hat_one, axis=0)
    shift_one_grad = jnp.sum(normed_grad, axis=0)
    first_grad = norm_back(normed_grad * gain_one, hat_one, inverse_one)
    attended_low = first_grad.astype(LOW)
    proj_grad = mm(context, attended_low, ((0,), (0,))).astype(LOW)
    proj_shift_grad = jnp.sum(attended_low.astype(F32), axis=0)
    context_grad = mm(attended_low, proj, ((1,), (1,))).astype(LOW).reshape(rows, slots, heads, DH)
    soft = soft_low.astype(F32)
    soft_grad = jnp.einsum("bqhd,bkhd->bhqk", context_grad, values, preferred_element_type=F32)
    score_low = (soft * (soft_grad - jnp.sum(soft * soft_grad, axis=-1, keepdims=True))).astype(LOW)
    query_grad = jnp.einsum("bhqk,bkhd->bqhd", score_low, keyset, preferred_element_type=F32) * DH**-0.5
    key_grad = jnp.einsum("bhqk,bqhd->bkhd", score_low, queries, preferred_element_type=F32) * DH**-0.5
    value_grad = jnp.einsum("bhqk,bqhd->bkhd", soft_low, context_grad, preferred_element_type=F32)
    packed_grad = jnp.stack([query_grad, key_grad, value_grad], axis=3).astype(LOW)
    shift_grad = jnp.sum(packed_grad.astype(F32), axis=(0, 1))
    qv_shift_grad = jnp.concatenate([shift_grad[:, 0], shift_grad[:, 2]], axis=1)
    packed_grad = packed_grad.reshape(count, groups, width)
    qkv_grad = jnp.einsum("nd,nge->gde", flat_tokens, packed_grad, preferred_element_type=F32).astype(LOW)
    input_grad = first_grad + jnp.einsum("nge,gde->nd", packed_grad, qkv, preferred_element_type=F32)
    input_grad = input_grad.astype(LOW).reshape(tokens.shape)
    grads = (
        qkv_grad, qv_shift_grad, proj_grad, proj_shift_grad, gain_one_grad, shift_one_grad,
        inner_grad, inner_shift_grad, outer_grad, outer_shift_grad, gain_two_grad, shift_two_grad,
    )
    return result, input_grad, grads


def on_device(*args):
    tokens, lengths, cotangent = args[:3]
    params = args[3:]
    qkv_weight, qv_shift, proj_weight, proj_shift, first_gain, first_shift = params[:6]
    inner_weight, inner_shift, outer_weight, outer_shift, second_gain, second_shift = params[6:]
    micro, local, slots, features = tokens.shape
    dp, groups = lax.axis_size("dp"), lax.axis_size("head")
    devices = dp * groups
    staged = (dp, groups) == (8, 4)
    position = lax.axis_index("head")
    me = device_index()
    own = lax.dynamic_slice_in_dim(lengths, position * local, local, 1).reshape(micro * local)
    rows = tokens.reshape(micro * local, slots, features)
    upstream = cotangent.reshape(micro * local, slots, features)
    depth, width = qkv_weight.shape
    hidden = inner_weight.shape[1]
    share = inner_weight.shape[0]

    vectors = [proj_shift, first_gain, first_shift, outer_shift, second_gain, second_shift, inner_shift, qv_shift.reshape(-1)]
    lens = [v.shape[0] for v in vectors]
    total = sum(lens)
    small = jnp.pad(jnp.concatenate(vectors).reshape(1, total), ((0, 7), (0, width - total)))

    if staged:
        def qkv_targets(source, refs, device):
            qkv_ref, small_ref = refs
            return [
                (source.at[pl.ds(0, depth)], qkv_ref.at[device % groups, device // groups]),
                (source.at[pl.ds(depth, 8)], small_ref.at[device]),
            ]

        qkv, small_all = assemble(
            jnp.concatenate([qkv_weight, small], axis=0), me,
            [jax.ShapeDtypeStruct((groups, dp, depth, width), LOW), jax.ShapeDtypeStruct((devices, 8, width), LOW)],
            qkv_targets,
        )
        qkv = qkv.reshape(groups, dp * depth, width)

        def inner_targets(source, refs, device):
            return [
                (source.at[:, pl.ds(0, hidden)], refs[0].at[device]),
                (source.at[:, pl.ds(hidden, features)], refs[1].at[device]),
            ]

        inner, proj = assemble(
            jnp.concatenate([inner_weight, proj_weight], axis=1), me,
            [jax.ShapeDtypeStruct((devices, share, hidden), LOW), jax.ShapeDtypeStruct((devices, share, features), LOW)],
            inner_targets,
        )
        (outer,) = assemble(
            outer_weight, me, [jax.ShapeDtypeStruct((devices,) + outer_weight.shape, LOW)],
            lambda source, refs, device: [(source, refs[0].at[device])],
        )
    else:
        def everyone(shard):
            return lax.all_gather(shard, AXES, axis=0)

        qkv = everyone(qkv_weight).reshape(dp, groups, depth, width).swapaxes(0, 1).reshape(groups, dp * depth, width)
        small_all, inner, proj, outer = everyone(small), everyone(inner_weight), everyone(proj_weight), everyone(outer_weight)
    inner, proj, outer = inner.reshape(features, hidden), proj.reshape(features, features), outer.reshape(hidden, features)
    pieces, at = [], 0
    for size in lens:
        pieces.append(small_all[:, 0, at : at + size].astype(F32))
        at += size
    full = [p.reshape(-1) for p in pieces[:-1]]
    shift = pieces[-1].reshape((dp, groups) + qv_shift.shape).transpose(1, 2, 0, 3).reshape(-1, 2 * DH)
    weights = (qkv, shift, proj, full[0], full[1], full[2], inner, full[6], outer, full[3], full[4], full[5])
    result, input_grad, grads = layer(rows, own, upstream, weights)
    (
        qkv_grad, qv_shift_grad, proj_grad, proj_shift_grad, gain_one_grad, shift_one_grad,
        inner_grad, inner_shift_grad, outer_grad, outer_shift_grad, gain_two_grad, shift_two_grad,
    ) = grads
    shift_blocks = qv_shift_grad.reshape(groups, qv_shift.shape[0], dp, qv_shift.shape[1]).transpose(2, 0, 1, 3)
    vector_grads = [proj_shift_grad, gain_one_grad, shift_one_grad, outer_shift_grad, gain_two_grad, shift_two_grad, inner_shift_grad, shift_blocks]
    small_grad = jnp.concatenate([g.reshape(devices, -1) for g in vector_grads], axis=1)
    small_grad = jnp.pad(small_grad.reshape(devices, 1, total), ((0, 0), (0, 7), (0, width - total)))
    outer_grad = outer_grad.reshape((devices,) + outer_weight.shape)
    inner_grad = inner_grad.reshape(devices, share, hidden)
    proj_grad = proj_grad.reshape(devices, share, features)
    qkv_grad = qkv_grad.reshape(groups, dp, depth, width)

    if staged:
        outer_out = reduce_parts(*split_parts(
            [outer_grad], me, outer_weight.shape, lambda refs, target, device: [(refs[0].at[device], target)]))
        inner_proj = reduce_parts(*split_parts(
            [inner_grad, proj_grad], me, (share, hidden + features),
            lambda refs, target, device: [
                (refs[0].at[device], target.at[:, pl.ds(0, hidden)]),
                (refs[1].at[device], target.at[:, pl.ds(hidden, features)]),
            ]))
        inner_out, proj_out = inner_proj[:, :hidden], inner_proj[:, hidden:]
        qkv_small = reduce_parts(*split_parts(
            [qkv_grad, small_grad.astype(LOW)], me, (depth + 8, width),
            lambda refs, target, device: [
                (refs[0].at[device % groups, device // groups], target.at[pl.ds(0, depth)]),
                (refs[1].at[device], target.at[pl.ds(depth, 8)]),
            ]))
        qkv_out, small_out = qkv_small[:depth], qkv_small[depth]
    else:
        def owner(grad):
            parts = lax.all_to_all(grad, AXES, 0, 0, tiled=True)
            return jnp.sum(parts.astype(F32), axis=0)

        outer_out, inner_out, proj_out = owner(outer_grad), owner(inner_grad), owner(proj_grad)
        qkv_out = owner(qkv_grad.swapaxes(0, 1).reshape(devices, depth, width))
        small_out = owner(small_grad)[0]
    outs, at = [], 0
    for size in lens:
        outs.append(small_out[at : at + size])
        at += size
    return (
        result.reshape(tokens.shape), input_grad.reshape(tokens.shape),
        qkv_out, outs[7].reshape(qv_shift.shape), proj_out, outs[0], outs[1], outs[2],
        inner_out, outs[6], outer_out, outs[3], outs[4], outs[5],
    )


def solution(mesh):
    both = ("dp", "head")
    rows, whole = P(both), P(both, None)
    data = P(None, both, None, None)
    params = (P("dp", "head"), P("head", "dp"), whole, rows, rows, rows, whole, rows, whole, rows, rows, rows)
    in_specs = (data, P(None, "dp"), data) + params
    out_specs = (data, data) + params
    return jax.shard_map(on_device, mesh=mesh, in_specs=in_specs, out_specs=out_specs, check_vma=False)
```
